1024 devices in a mesh: outer: 32 (over z, core), inner: 8 (over x, y_lo), head: 4 (over y_hi).
Axes of the slice: x: 4, y: 8 (y_hi: 4, y_lo: 2; y = y_hi * 2 + y_lo), z: 16, core: 2. Of those that a mesh axis runs over, the one named last changes fastest.
Arguments:
- queries: bfloat16 [65536, 4096], P(('outer', 'inner', 'head')), may hold values from -6 to 6
- keys: bfloat16 [65536, 512], P(('outer', 'inner', 'head')), may hold values from -6 to 6
- values: bfloat16 [65536, 512], P(('outer', 'inner', 'head')), may hold values from -6 to 6
- doc_lengths: int32 [4096], replicated, may hold values from 1 to 256, 65536 in all
Outputs:
- attended: bfloat16 [65536, 4096], P(('outer', 'inner', 'head'))
The draws below stay inside these ranges and needn't reach their ends.
Inputs may be any that keep to these rules, and one draw needn't show every extreme that they name: `doc_lengths`: the documents lie end to end in order of position; the lengths sum to 65536 and the largest is exactly 256.
All inputs are finite; a program needn't handle non-finite values.
Results may differ from the reference program's by a relative error of at most 0.0019.
Values may be sent and summed in bfloat16 or wider, within the bound.
No kernel may reach another device: no remote copies, remote signals or barrier semaphores. Data moves between devices by JAX's collectives and lax.ppermute only.
A program may use at most 32 MiB of HBM per device.

```python
import math
import jax
import jax.numpy as jnp
import numpy as np
from jax import lax

QUERY_HEAD_COUNT = 32
KEY_VALUE_HEADS = 4
HEAD_WIDTH = 128
BLOCK_TOKENS = 128
DOCUMENT_SPAN = 2
QUERY_PER_KEY = 8
SEQUENCE_TOKENS = 65536
MAXDOC = 256
NDOC = 4096
N_OUTER = 32
N_INNER = 8


def draw_keys(key, part):
    attention_output = jnp.clip(jax.random.normal(jax.random.fold_in(key, 2), (SEQUENCE_TOKENS, KEY_VALUE_HEADS * HEAD_WIDTH), jnp.float32), -4.0, 4.0)
    return attention_output.astype(jnp.bfloat16)


def draw_queries(key, part):
    attention_output = jnp.clip(jax.random.normal(jax.random.fold_in(key, 1), (SEQUENCE_TOKENS, QUERY_HEAD_COUNT * HEAD_WIDTH), jnp.float32), -4.0, 4.0)
    return attention_output.astype(jnp.bfloat16)


def block_levels(key, extent, split, least, high):
    loudness, own = 1.0, jax.random.fold_in(key, 6)
    for axis_at, shards_of in split:
        heights = jnp.exp(jax.random.uniform(jax.random.fold_in(own, axis_at), (shards_of,), jnp.float32, least / len(split), high / len(split)))
        loudness = loudness * jnp.repeat(heights, extent[axis_at] // shards_of).reshape([-1 if axis == axis_at else 1 for axis in range(len(extent))])
    return loudness


def split_up(count, total, most, skew):
    loads = [(1 << 20) // math.isqrt(standing ** skew) + 1 for standing in range(2, count + 1)]
    surplus, counts = total - most - (count - 1), [1] * (count - 1)
    while surplus > 0:
        movable = [i for i in range(count - 1) if counts[i] < most]
        whole, left = sum([loads[i] for i in movable]), surplus
        for i in movable:
            more = min(most - counts[i], max(1, left * loads[i] // whole), surplus)
            counts[i] = counts[i] + more
            surplus = surplus - more
    return np.array([most] + counts)


def ragged(stream_key, amount, total, most, slope):
    if amount == 2:
        one = jax.random.randint(stream_key, (), max(1, total - most), min(most, total - 1) + 1)
        return jnp.stack([one, total - one])
    sizes = jnp.asarray(split_up(amount, total, most, slope), jnp.int32)
    couples = (amount - 1) // 2
    source_of, receiver = sizes[1:1 + 2 * couples:2], sizes[2:2 + 2 * couples:2]
    margin = jnp.minimum(source_of - 1, most - receiver)
    passed = jax.random.randint(jax.random.fold_in(stream_key, 1), (couples,), 0, 1 << 20) % (margin + 1)
    sizes = sizes.at[1:1 + 2 * couples:2].set(source_of - passed).at[2:2 + 2 * couples:2].set(receiver + passed)
    return sizes[jax.random.permutation(jax.random.fold_in(stream_key, 2), amount)]


def noise(rng, extent, scale, most, split=(), held_as=jnp.bfloat16):
    values = jax.random.normal(rng, extent, jnp.float32) * scale
    if len(split) > 0:
        values = block_levels(rng, extent, split, -0.22, 0.18) * values
    return jnp.clip(values, min=-most, max=most).astype(held_as)


def setup_inputs(seed: int = 0) -> dict:
    seeds = jax.random.split(jax.random.key(seed), 5)
    return {
        "queries": draw_queries(jax.random.fold_in(seeds[4], 71), 0),
        "keys": draw_keys(jax.random.fold_in(seeds[4], 71), 0),
        "values": noise(seeds[2], (SEQUENCE_TOKENS, KEY_VALUE_HEADS * HEAD_WIDTH), 1.0, 6.0, ((0, 1024),)),
        "doc_lengths": ragged(seeds[3], NDOC, SEQUENCE_TOKENS, MAXDOC, 2).astype(jnp.int32),
    }


NEG = -1e+30

def sorted_ordering(array, context_block_count):
    halves = array.reshape(context_block_count, 2, BLOCK_TOKENS, array.shape[-1])
    return jnp.concatenate([halves[:, 0], halves[::-1, 1]], axis=0)

def reference(queries, keys, values, doc_lengths):
    context_block_count = N_OUTER * N_INNER
    segment_count = 2 * context_block_count
    query_segments = sorted_ordering(queries, context_block_count).reshape(segment_count, BLOCK_TOKENS, KEY_VALUE_HEADS, QUERY_PER_KEY, HEAD_WIDTH)
    key_stretches = sorted_ordering(keys, context_block_count)
    value_stretches = sorted_ordering(values, context_block_count)
    padding_amount = jnp.zeros((DOCUMENT_SPAN, BLOCK_TOKENS, KEY_VALUE_HEADS * HEAD_WIDTH), keys.dtype)
    key_with_padding = jnp.concatenate([padding_amount, key_stretches], axis=0)
    value_with_padding = jnp.concatenate([padding_amount, value_stretches], axis=0)
    doc_ends = jnp.cumsum(doc_lengths).astype(jnp.int32)
    positions = jnp.arange(SEQUENCE_TOKENS, dtype=jnp.int32)
    doc_ids = jnp.searchsorted(doc_ends, positions, side='right').astype(jnp.int32).reshape(segment_count, BLOCK_TOKENS)
    doc_padded = jnp.concatenate([jnp.full((DOCUMENT_SPAN, BLOCK_TOKENS), -1, jnp.int32), doc_ids], axis=0)
    visible_span = (DOCUMENT_SPAN + 1) * BLOCK_TOKENS
    offsets = jnp.arange(BLOCK_TOKENS, dtype=jnp.int32)
    spread = jnp.arange(visible_span, dtype=jnp.int32)
    score_scale = 1.0 / math.sqrt(HEAD_WIDTH)

    def one_stretch(segment_index):
        query_block = lax.dynamic_index_in_dim(query_segments, segment_index, 0, keepdims=False).astype(jnp.float32)
        key_tile_rows = lax.dynamic_slice_in_dim(key_with_padding, segment_index, DOCUMENT_SPAN + 1, 0).reshape(visible_span, KEY_VALUE_HEADS, HEAD_WIDTH).astype(jnp.float32)
        value_tile_rows = lax.dynamic_slice_in_dim(value_with_padding, segment_index, DOCUMENT_SPAN + 1, 0).reshape(visible_span, KEY_VALUE_HEADS, HEAD_WIDTH).astype(jnp.float32)
        key_docs = lax.dynamic_slice_in_dim(doc_padded, segment_index, DOCUMENT_SPAN + 1, 0).reshape(visible_span)
        query_docs = lax.dynamic_index_in_dim(doc_ids, segment_index, 0, keepdims=False)
        query_positions = segment_index * BLOCK_TOKENS + offsets
        key_positions = (segment_index - DOCUMENT_SPAN) * BLOCK_TOKENS + spread
        allowed = (query_docs[:, None] == key_docs[None, :]) & (key_positions[None, :] <= query_positions[:, None])
        scores = jnp.einsum('qhgd,khd->hgqk', query_block, key_tile_rows) * score_scale
        scores = jnp.where(allowed, scores, NEG)
        maximum = lax.optimization_barrier(jnp.max(scores, axis=-1, keepdims=True))
        weights = jnp.where(allowed, jnp.exp(scores - maximum), 0.0)
        totals = lax.optimization_barrier(jnp.sum(weights, axis=-1))
        rounded = lax.optimization_barrier(weights.astype(jnp.bfloat16)).astype(jnp.float32)
        summed = jnp.einsum('hgqk,khd->hgqd', rounded, value_tile_rows)
        attention_output = (summed / totals[..., None]).transpose(2, 0, 1, 3)
        return attention_output.reshape(BLOCK_TOKENS, QUERY_HEAD_COUNT * HEAD_WIDTH).astype(jnp.bfloat16)
    attended = lax.map(one_stretch, jnp.arange(segment_count, dtype=jnp.int32))
    front = attended[:context_block_count]
    behind = attended[context_block_count:][::-1]
    return jnp.stack([front, behind], axis=1).reshape(SEQUENCE_TOKENS, QUERY_HEAD_COUNT * HEAD_WIDTH)
```

```python
import functools
import math

import jax
import jax.numpy as jnp
from jax import lax
from jax.experimental import pallas as pl
from jax.experimental.pallas import tpu as pltpu
from jax.sharding import PartitionSpec as P

HEAD_WIDTH = 128
QUERY_PER_KEY = 8
MAXDOC = 256
LANES = 128
NEG = -1e30
AXES = ("outer", "inner", "head")


def chunk_of(device, blocks):
    block, part = divmod(device, 4)
    return 2 * block + part if part < 2 else 4 * blocks - 4 - 2 * block + part


def bias_kernel(rows, back, base_ref, len_ref, bias_ref):
    base = base_ref[0]
    ends = len_ref[...]
    lane = lax.broadcasted_iota(jnp.int32, ends.shape, 1)
    shift = 1
    while shift < LANES:
        ends = ends + jnp.where(lane >= shift, pltpu.roll(ends, shift, 1), 0)
        shift *= 2
    totals = jnp.broadcast_to(ends[:, LANES - 1 :], ends.shape)
    row = lax.broadcasted_iota(jnp.int32, ends.shape, 0)
    above = jnp.where(row >= 1, pltpu.roll(totals, 1, 0), 0)
    shift = 1
    while shift < ends.shape[0]:
        above = above + jnp.where(row >= shift, pltpu.roll(above, shift, 0), 0)
        shift *= 2
    ends = ends + above
    own = base + lax.broadcasted_iota(jnp.int32, (rows, LANES), 0)
    first = jnp.zeros((rows, LANES), jnp.int32)
    for i in range(ends.shape[0]):
        end = jnp.broadcast_to(ends[i : i + 1, :], (rows, LANES))
        first = jnp.maximum(first, jnp.where(end <= own, end, 0))
    first = jnp.max(first, axis=1, keepdims=True)
    column = lax.broadcasted_iota(jnp.int32, bias_ref.shape, 1) + (base - back)
    mine = lax.broadcasted_iota(jnp.int32, bias_ref.shape, 0) + base
    bias_ref[...] = jnp.where((column >= first) & (column <= mine), 0.0, NEG)


def attend_kernel(scale, q_ref, *refs):
    count = (len(refs) - 2) // 2
    key_refs, value_refs = refs[:count], refs[count : 2 * count]
    bias_ref, out_ref = refs[2 * count :]
    rows = q_ref.shape[0]
    heads = q_ref.shape[1] // HEAD_WIDTH
    q = jnp.concatenate([q_ref[:, j * HEAD_WIDTH : (j + 1) * HEAD_WIDTH] for j in range(heads)], axis=0)
    k = jnp.concatenate([r[...] for r in key_refs], axis=0)
    v = jnp.concatenate([r[...] for r in value_refs], axis=0)
    s = lax.dot_general(q, k, (((1,), (1,)), ((), ())), preferred_element_type=jnp.float32)
    s = s * scale + jnp.concatenate([bias_ref[...]] * heads, axis=0)
    w = jnp.exp(s - jnp.max(s, axis=1, keepdims=True))
    z = jnp.sum(w, axis=1, keepdims=True)
    o = jnp.dot(w.astype(jnp.bfloat16), v, preferred_element_type=jnp.float32)
    o = (o / z).astype(out_ref.dtype)
    for j in range(heads):
        out_ref[:, j * HEAD_WIDTH : (j + 1) * HEAD_WIDTH] = o[j * rows : (j + 1) * rows]


def local(queries, keys, values, doc_lengths):
    rows, width = keys.shape
    key_heads = width // HEAD_WIDTH
    back = MAXDOC
    steps = back // rows
    blocks = lax.axis_size("outer") * lax.axis_size("inner")
    count = 4 * blocks
    device_of = {chunk_of(d, blocks): d for d in range(count)}
    own = jnp.concatenate([keys, values], axis=1)
    got = [
        lax.ppermute(own, AXES, [(device_of[k], device_of[(k + step) % count]) for k in range(count)])
        for step in range(steps, 0, -1)
    ] + [own]

    block = lax.axis_index("outer") * lax.axis_size("inner") + lax.axis_index("inner")
    part = lax.axis_index("head")
    chunk = jnp.where(part < 2, 2 * block + part, count - 4 - 2 * block + part)
    base = jnp.reshape(chunk * rows, (1,)).astype(jnp.int32)
    bias = pl.pallas_call(
        functools.partial(bias_kernel, rows, back),
        out_shape=jax.ShapeDtypeStruct((rows, back + rows), jnp.float32),
        in_specs=[pl.BlockSpec(memory_space=pltpu.SMEM), pl.BlockSpec(memory_space=pltpu.VMEM)],
        out_specs=pl.BlockSpec(memory_space=pltpu.VMEM),
        cost_estimate=pl.CostEstimate(flops=2_000_000, bytes_accessed=100_000, transcendentals=0),
        compiler_params=pltpu.CompilerParams(vmem_limit_bytes=16 << 20),
        name="bias",
    )(base, doc_lengths.reshape(-1, LANES))

    per_head = QUERY_PER_KEY * HEAD_WIDTH
    return pl.pallas_call(
        functools.partial(attend_kernel, 1.0 / math.sqrt(HEAD_WIDTH)),
        out_shape=jax.ShapeDtypeStruct(queries.shape, queries.dtype),
        grid=(key_heads,),
        in_specs=[pl.BlockSpec((rows, per_head), lambda g: (0, g))]
        + [pl.BlockSpec((rows, HEAD_WIDTH), lambda g: (0, g))] * len(got)
        + [pl.BlockSpec((rows, HEAD_WIDTH), lambda g: (0, key_heads + g))] * len(got)
        + [pl.BlockSpec((rows, back + rows), lambda g: (0, 0))],
        out_specs=pl.BlockSpec((rows, per_head), lambda g: (0, g)),
        cost_estimate=pl.CostEstimate(flops=400_000_000, bytes_accessed=2_000_000, transcendentals=700_000),
        compiler_params=pltpu.CompilerParams(vmem_limit_bytes=16 << 20),
        name="attend",
    )(queries, *got, *got, bias)


def solution(mesh):
    return jax.shard_map(
        local,
        mesh=mesh,
        in_specs=(P(AXES, None), P(AXES, None), P(AXES, None), P()),
        out_specs=P(AXES, None),
        check_vma=False,
    )
```

```python
import functools
import math

import jax
import jax.numpy as jnp
from jax import lax
from jax.experimental import pallas as pl
from jax.experimental.pallas import tpu as pltpu
from jax.sharding import PartitionSpec as P

HEAD_WIDTH = 128
QUERY_PER_KEY = 8
MAXDOC = 256
LANES = 128
NEG = -1e30
AXES = ("outer", "inner", "head")


def chunk_of(device, blocks):
    block, part = divmod(device, 4)
    return 2 * block + part if part < 2 else 4 * blocks - 4 - 2 * block + part


def bias_kernel(rows, back, base_ref, len_ref, bias_ref):
    base = base_ref[0]
    ends = len_ref[...]
    lane = lax.broadcasted_iota(jnp.int32, ends.shape, 1)
    shift = 1
    while shift < LANES:
        ends = ends + jnp.where(lane >= shift, pltpu.roll(ends, shift, 1), 0)
        shift *= 2
    totals = jnp.broadcast_to(ends[:, LANES - 1 :], ends.shape)
    row = lax.broadcasted_iota(jnp.int32, ends.shape, 0)
    above = jnp.where(row >= 1, pltpu.roll(totals, 1, 0), 0)
    shift = 1
    while shift < ends.shape[0]:
        above = above + jnp.where(row >= shift, pltpu.roll(above, shift, 0), 0)
        shift *= 2
    ends = ends + above
    own = base + lax.broadcasted_iota(jnp.int32, (rows, LANES), 0)
    first = jnp.zeros((rows, LANES), jnp.int32)
    for i in range(ends.shape[0]):
        end = jnp.broadcast_to(ends[i : i + 1, :], (rows, LANES))
        first = jnp.maximum(first, jnp.where(end <= own, end, 0))
    first = jnp.max(first, axis=1, keepdims=True)
    column = lax.broadcasted_iota(jnp.int32, bias_ref.shape, 1) + (base - back)
    mine = lax.broadcasted_iota(jnp.int32, bias_ref.shape, 0) + base
    bias_ref[...] = jnp.where((column >= first) & (column <= mine), 0.0, NEG)


def attend_kernel(scale, q_ref, *refs):
    count = (len(refs) - 2) // 2
    key_refs, value_refs = refs[:count], refs[count : 2 * count]
    bias_ref, out_ref = refs[2 * count :]
    rows = q_ref.shape[0]
    heads = q_ref.shape[1] // HEAD_WIDTH
    q = jnp.concatenate([q_ref[:, j * HEAD_WIDTH : (j + 1) * HEAD_WIDTH] for j in range(heads)], axis=0)
    k = jnp.concatenate([r[...] for r in key_refs], axis=0)
    v = jnp.concatenate([r[...] for r in value_refs], axis=0)
    s = lax.dot_general(q, k, (((1,), (1,)), ((), ())), preferred_element_type=jnp.float32)
    s = s * scale + jnp.concatenate([bias_ref[...]] * heads, axis=0)
    w = jnp.exp(s - jnp.max(s, axis=1, keepdims=True))
    z = jnp.sum(w, axis=1, keepdims=True)
    o = jnp.dot(w.astype(jnp.bfloat16), v, preferred_element_type=jnp.float32)
    o = (o / z).astype(out_ref.dtype)
    for j in range(heads):
        out_ref[:, j * HEAD_WIDTH : (j + 1) * HEAD_WIDTH] = o[j * rows : (j + 1) * rows]


def local(queries, keys, values, doc_lengths):
    rows, width = keys.shape
    key_heads = width // HEAD_WIDTH
    back = MAXDOC
    steps = back // rows
    blocks = lax.axis_size("outer") * lax.axis_size("inner")
    count = 4 * blocks
    device_of = {chunk_of(d, blocks): d for d in range(count)}
    own = jnp.concatenate([keys, values], axis=1)
    got = [
        lax.ppermute(own, AXES, [(device_of[k], device_of[k + step]) for k in range(count - step)])
        for step in range(steps, 0, -1)
    ] + [own]

    block = lax.axis_index("outer") * lax.axis_size("inner") + lax.axis_index("inner")
    part = lax.axis_index("head")
    chunk = jnp.where(part < 2, 2 * block + part, count - 4 - 2 * block + part)
    base = jnp.reshape(chunk * rows, (1,)).astype(jnp.int32)
    bias = pl.pallas_call(
        functools.partial(bias_kernel, rows, back),
        out_shape=jax.ShapeDtypeStruct((rows, back + rows), jnp.float32),
        in_specs=[pl.BlockSpec(memory_space=pltpu.SMEM), pl.BlockSpec(memory_space=pltpu.VMEM)],
        out_specs=pl.BlockSpec(memory_space=pltpu.VMEM),
        cost_estimate=pl.CostEstimate(flops=2_000_000, bytes_accessed=100_000, transcendentals=0),
        compiler_params=pltpu.CompilerParams(vmem_limit_bytes=16 << 20),
        name="bias",
    )(base, doc_lengths.reshape(-1, LANES))

    per_head = QUERY_PER_KEY * HEAD_WIDTH
    return pl.pallas_call(
        functools.partial(attend_kernel, 1.0 / math.sqrt(HEAD_WIDTH)),
        out_shape=jax.ShapeDtypeStruct(queries.shape, queries.dtype),
        grid=(key_heads,),
        in_specs=[pl.BlockSpec((rows, per_head), lambda g: (0, g))]
        + [pl.BlockSpec((rows, HEAD_WIDTH), lambda g: (0, g))] * len(got)
        + [pl.BlockSpec((rows, HEAD_WIDTH), lambda g: (0, key_heads + g))] * len(got)
        + [pl.BlockSpec((rows, back + rows), lambda g: (0, 0))],
        out_specs=pl.BlockSpec((rows, per_head), lambda g: (0, g)),
        cost_estimate=pl.CostEstimate(flops=400_000_000, bytes_accessed=2_000_000, transcendentals=700_000),
        compiler_params=pltpu.CompilerParams(vmem_limit_bytes=16 << 20),
        name="attend",
    )(queries, *got, *got, bias)


def solution(mesh):
    return jax.shard_map(
        local,
        mesh=mesh,
        in_specs=(P(AXES, None), P(AXES, None), P(AXES, None), P()),
        out_specs=P(AXES, None),
        check_vma=False,
    )
```

```python
import functools
import math

import jax
import jax.numpy as jnp
from jax import lax
from jax.experimental import pallas as pl
from jax.experimental.pallas import tpu as pltpu
from jax.sharding import PartitionSpec as P

HEAD_WIDTH = 128
QUERY_PER_KEY = 8
MAXDOC = 256
LANES = 128
NEG = -1e30
AXES = ("outer", "inner", "head")
VMEM = pl.BlockSpec(memory_space=pltpu.VMEM)
SMEM = pl.BlockSpec(memory_space=pltpu.SMEM)
ANY = pl.BlockSpec(memory_space=pl.ANY)
HBM = pl.BlockSpec(memory_space=pltpu.HBM)
PARAMS = pltpu.CompilerParams(vmem_limit_bytes=16 << 20)


def in_hbm(array):
    return pltpu.with_memory_space_constraint(array, pltpu.HBM)


def chunk_of(device, blocks):
    block, part = divmod(device, 4)
    return 2 * block + part if part < 2 else 4 * blocks - 4 - 2 * block + part


def join_kernel(k_ref, v_ref, out_ref, sem):
    rows = k_ref.shape[0]
    copies = [
        pltpu.make_async_copy(k_ref, out_ref.at[pl.ds(0, rows)], sem.at[0]),
        pltpu.make_async_copy(v_ref, out_ref.at[pl.ds(rows, rows)], sem.at[1]),
    ]
    for copy in copies:
        copy.start()
    for copy in copies:
        copy.wait()


def first_positions(base, lengths, rows):
    ends = lengths
    lane = lax.broadcasted_iota(jnp.int32, ends.shape, 1)
    shift = 1
    while shift < LANES:
        ends = ends + jnp.where(lane >= shift, pltpu.roll(ends, shift, 1), 0)
        shift *= 2
    totals = jnp.broadcast_to(ends[:, LANES - 1 :], ends.shape)
    row = lax.broadcasted_iota(jnp.int32, ends.shape, 0)
    above = jnp.where(row >= 1, pltpu.roll(totals, 1, 0), 0)
    shift = 1
    while shift < ends.shape[0]:
        above = above + jnp.where(row >= shift, pltpu.roll(above, shift, 0), 0)
        shift *= 2
    ends = ends + above
    own = base + lax.broadcasted_iota(jnp.int32, (rows, LANES), 0)
    first = jnp.zeros((rows, LANES), jnp.int32)
    for i in range(ends.shape[0]):
        end = jnp.broadcast_to(ends[i : i + 1, :], (rows, LANES))
        first = jnp.maximum(first, jnp.where(end <= own, end, 0))
    first = jnp.broadcast_to(jnp.max(first, axis=1, keepdims=True), (rows, LANES))
    return jnp.concatenate([first] * (LANES // rows), axis=0).T


def queries_of(q_ref, g):
    start = g * QUERY_PER_KEY * HEAD_WIDTH
    return jnp.concatenate(
        [q_ref[:, start + j * HEAD_WIDTH : start + (j + 1) * HEAD_WIDTH] for j in range(QUERY_PER_KEY)],
        axis=0,
    )


def part_of(refs, half, g):
    rows = refs[0].shape[0] // 2
    return jnp.concatenate(
        [r[half * rows : (half + 1) * rows, g * HEAD_WIDTH : (g + 1) * HEAD_WIDTH] for r in refs], axis=0
    )


def scores_of(q_ref, refs, g, bias, scale):
    q = queries_of(q_ref, g)
    s = lax.dot_general(
        part_of(refs, 0, g), q, (((1,), (1,)), ((), ())), preferred_element_type=jnp.float32
    )
    return s * scale + jnp.concatenate([bias] * (q.shape[0] // LANES), axis=1)


def weighted(refs, g, w):
    return lax.dot_general(
        part_of(refs, 1, g),
        w.astype(jnp.bfloat16),
        (((0,), (0,)), ((), ())),
        preferred_element_type=jnp.float32,
    )


def near_kernel(scale, near, base_ref, len_ref, q_hbm_ref, *refs):
    kv_refs = refs[:near]
    q_ref, bias_ref, top_ref, total_ref, sum_ref, sem = refs[near:]
    copy = pltpu.make_async_copy(q_hbm_ref, q_ref, sem)
    copy.start()
    rows = q_ref.shape[0]
    base = base_ref[0]
    first = first_positions(base, len_ref[...], rows)
    far = bias_ref.shape[0]
    count = far + near * rows
    first = jnp.broadcast_to(first[:1], (count, LANES))
    lane = lax.broadcasted_iota(jnp.int32, (count, LANES), 1)
    column = lax.broadcasted_iota(jnp.int32, (count, LANES), 0) + (base + rows - count)
    bias = jnp.where((column >= first) & (column <= base + lane % rows), 0.0, NEG)
    bias_ref[...] = bias[:far]
    copy.wait()
    for g in range(sum_ref.shape[0]):
        s = scores_of(q_ref, kv_refs, g, bias[far:], scale)
        top = jnp.max(s, axis=0, keepdims=True)
        w = jnp.exp(s - top)
        top_ref[g] = top
        total_ref[g] = jnp.sum(w, axis=0, keepdims=True)
        sum_ref[g] = weighted(kv_refs, g, w)


def far_kernel(scale, far, q_ref, bias_ref, top_ref, total_ref, sum_ref, *refs):
    kv_refs = refs[:far]
    out_ref, held, sem = refs[far:]
    rows = q_ref.shape[0]
    width = QUERY_PER_KEY * HEAD_WIDTH
    copies = []
    for g in range(sum_ref.shape[0]):
        s = scores_of(q_ref, kv_refs, g, bias_ref[...], scale)
        top = jnp.maximum(top_ref[g], jnp.max(s, axis=0, keepdims=True))
        w = jnp.exp(s - top)
        rescale = jnp.exp(top_ref[g] - top)
        total = rescale * total_ref[g] + jnp.sum(w, axis=0, keepdims=True)
        o = (rescale * sum_ref[g] + weighted(kv_refs, g, w)) * (1.0 / total)
        o = o.T.astype(held.dtype)
        for j in range(QUERY_PER_KEY):
            held[g, :, j * HEAD_WIDTH : (j + 1) * HEAD_WIDTH] = o[j * rows : (j + 1) * rows]
        copy = pltpu.make_async_copy(held.at[g], out_ref.at[:, pl.ds(g * width, width)], sem.at[g])
        copy.start()
        copies.append(copy)
    for copy in copies:
        copy.wait()


def local(queries, keys, values, doc_lengths):
    rows, width = keys.shape
    key_heads = width // HEAD_WIDTH
    steps = MAXDOC // rows
    near, far = steps // 2 + 1, steps // 2
    blocks = lax.axis_size("outer") * lax.axis_size("inner")
    count = 4 * blocks
    device_of = {chunk_of(d, blocks): d for d in range(count)}
    own = pl.pallas_call(
        join_kernel,
        out_shape=jax.ShapeDtypeStruct((2 * rows, width), keys.dtype),
        in_specs=[HBM, HBM],
        out_specs=ANY,
        scratch_shapes=[pltpu.SemaphoreType.DMA((2,))],
        compiler_params=PARAMS,
        name="join",
    )(in_hbm(keys), in_hbm(values))
    got = {
        step: lax.ppermute(own, AXES, [(device_of[k], device_of[k + step]) for k in range(count - step)])
        for step in range(1, steps + 1)
    }

    block = lax.axis_index("outer") * lax.axis_size("inner") + lax.axis_index("inner")
    part = lax.axis_index("head")
    chunk = jnp.where(part < 2, 2 * block + part, count - 4 - 2 * block + part)
    base = jnp.reshape(chunk * rows, (1,)).astype(jnp.int32)
    scale = 1.0 / math.sqrt(HEAD_WIDTH)
    heads_rows = QUERY_PER_KEY * rows
    row = jax.ShapeDtypeStruct((key_heads, 1, heads_rows), jnp.float32)
    state = pl.pallas_call(
        functools.partial(near_kernel, scale, near),
        out_shape=(
            jax.ShapeDtypeStruct(queries.shape, queries.dtype),
            jax.ShapeDtypeStruct((far * rows, LANES), jnp.float32),
            row,
            row,
            jax.ShapeDtypeStruct((key_heads, HEAD_WIDTH, heads_rows), jnp.float32),
        ),
        in_specs=[SMEM, VMEM, HBM] + [VMEM] * near,
        out_specs=(VMEM,) * 5,
        scratch_shapes=[pltpu.SemaphoreType.DMA],
        cost_estimate=pl.CostEstimate(flops=240_000_000, bytes_accessed=2_000_000, transcendentals=400_000),
        compiler_params=PARAMS,
        name="near",
    )(base, doc_lengths.reshape(-1, LANES), in_hbm(queries), *[got[s] for s in range(near - 1, 0, -1)], own)

    return pl.pallas_call(
        functools.partial(far_kernel, scale, far),
        out_shape=jax.ShapeDtypeStruct(queries.shape, queries.dtype),
        in_specs=[VMEM] * (5 + far),
        out_specs=ANY,
        scratch_shapes=[
            pltpu.VMEM((key_heads, rows, QUERY_PER_KEY * HEAD_WIDTH), queries.dtype),
            pltpu.SemaphoreType.DMA((key_heads,)),
        ],
        cost_estimate=pl.CostEstimate(flops=160_000_000, bytes_accessed=2_000_000, transcendentals=300_000),
        compiler_params=PARAMS,
        name="far",
    )(*state, *[got[s] for s in range(steps, near - 1, -1)])


def solution(mesh):
    return jax.shard_map(
        local,
        mesh=mesh,
        in_specs=(P(AXES, None), P(AXES, None), P(AXES, None), P()),
        out_specs=P(AXES, None),
        check_vma=False,
    )
```

```python
import functools
import math

import jax
import jax.numpy as jnp
from jax import lax
from jax.experimental import pallas as pl
from jax.experimental.pallas import tpu as pltpu
from jax.sharding import PartitionSpec as P

HEAD_WIDTH = 128
QUERY_PER_KEY = 8
MAXDOC = 256
LANES = 128
NEG = -1e30
SENT = (3, 2, 1, 4)
NEAR = (3, 0)
MIDS = ((1,), (2,))
FAR = (4,)
AXES = ("outer", "inner", "head")
VMEM = pl.BlockSpec(memory_space=pltpu.VMEM)
SMEM = pl.BlockSpec(memory_space=pltpu.SMEM)
ANY = pl.BlockSpec(memory_space=pl.ANY)
HBM = pl.BlockSpec(memory_space=pltpu.HBM)
PARAMS = pltpu.CompilerParams(vmem_limit_bytes=16 << 20)


def in_hbm(array):
    return pltpu.with_memory_space_constraint(array, pltpu.HBM)


def chunk_of(device, blocks):
    block, part = divmod(device, 4)
    return 2 * block + part if part < 2 else 4 * blocks - 4 - 2 * block + part


def join_kernel(k_ref, v_ref, out_ref, sem):
    rows = k_ref.shape[0]
    copies = [
        pltpu.make_async_copy(k_ref, out_ref.at[pl.ds(0, rows)], sem.at[0]),
        pltpu.make_async_copy(v_ref, out_ref.at[pl.ds(rows, rows)], sem.at[1]),
    ]
    for copy in copies:
        copy.start()
    for copy in copies:
        copy.wait()


def first_positions(base, lengths, rows):
    ends = lengths
    lane = lax.broadcasted_iota(jnp.int32, ends.shape, 1)
    shift = 1
    while shift < LANES:
        ends = ends + jnp.where(lane >= shift, pltpu.roll(ends, shift, 1), 0)
        shift *= 2
    totals = jnp.broadcast_to(ends[:, LANES - 1 :], ends.shape)
    row = lax.broadcasted_iota(jnp.int32, ends.shape, 0)
    above = jnp.where(row >= 1, pltpu.roll(totals, 1, 0), 0)
    shift = 1
    while shift < ends.shape[0]:
        above = above + jnp.where(row >= shift, pltpu.roll(above, shift, 0), 0)
        shift *= 2
    ends = ends + above
    own = base + lax.broadcasted_iota(jnp.int32, (rows, LANES), 0)
    first = jnp.zeros((rows, LANES), jnp.int32)
    for i in range(ends.shape[0]):
        end = jnp.broadcast_to(ends[i : i + 1, :], (rows, LANES))
        first = jnp.maximum(first, jnp.where(end <= own, end, 0))
    first = jnp.broadcast_to(jnp.max(first, axis=1, keepdims=True), (rows, LANES))
    return jnp.concatenate([first] * (LANES // rows), axis=0).T


def queries_of(q_ref, g):
    start = g * QUERY_PER_KEY * HEAD_WIDTH
    return jnp.concatenate(
        [q_ref[:, start + j * HEAD_WIDTH : start + (j + 1) * HEAD_WIDTH] for j in range(QUERY_PER_KEY)],
        axis=0,
    )


def part_of(refs, half, g):
    rows = refs[0].shape[0] // 2
    return jnp.concatenate(
        [r[half * rows : (half + 1) * rows, g * HEAD_WIDTH : (g + 1) * HEAD_WIDTH] for r in refs], axis=0
    )


def bias_of(bias_ref, steps, rows):
    count = bias_ref.shape[0]
    return jnp.concatenate([bias_ref[count - (n + 1) * rows : count - n * rows] for n in steps], axis=0)


def scores_of(q_ref, refs, g, bias, scale):
    q = queries_of(q_ref, g)
    s = lax.dot_general(
        part_of(refs, 0, g), q, (((1,), (1,)), ((), ())), preferred_element_type=jnp.float32
    )
    return s * scale + jnp.concatenate([bias] * (q.shape[0] // LANES), axis=1)


def weighted(refs, g, w):
    return lax.dot_general(
        part_of(refs, 1, g),
        w,
        (((0,), (0,)), ((), ())),
        preferred_element_type=jnp.float32,
    )


def near_kernel(scale, near, base_ref, len_ref, q_hbm_ref, *refs):
    kv_refs = refs[: len(near)]
    q_ref, bias_ref, top_ref, total_ref, sum_ref, sem = refs[len(near) :]
    copy = pltpu.make_async_copy(q_hbm_ref, q_ref, sem)
    copy.start()
    rows = q_ref.shape[0]
    base = base_ref[0]
    first = first_positions(base, len_ref[...], rows)
    count = bias_ref.shape[0]
    first = jnp.broadcast_to(first[:1], (count, LANES))
    lane = lax.broadcasted_iota(jnp.int32, (count, LANES), 1)
    column = lax.broadcasted_iota(jnp.int32, (count, LANES), 0) + (base + rows - count)
    bias_ref[...] = jnp.where((column >= first) & (column <= base + lane % rows), 0.0, NEG)
    bias = bias_of(bias_ref, near, rows)
    copy.wait()
    for g in range(sum_ref.shape[0]):
        s = scores_of(q_ref, kv_refs, g, bias, scale)
        top = jnp.max(s, axis=0, keepdims=True)
        w = jnp.exp2(s - top)
        top_ref[g] = top
        total_ref[g] = jnp.sum(w, axis=0, keepdims=True)
        sum_ref[g] = weighted(kv_refs, g, w.astype(jnp.bfloat16))


def mid_kernel(scale, steps, q_ref, bias_ref, top_ref, total_ref, sum_ref, *refs):
    kv_refs = refs[: len(steps)]
    new_top_ref, new_total_ref, new_sum_ref, score_ref, weight_ref = refs[len(steps) :]
    bias = bias_of(bias_ref, steps, q_ref.shape[0])
    heads = range(sum_ref.shape[0])
    for g in heads:
        score_ref[g] = scores_of(q_ref, kv_refs, g, bias, scale)
    rescales = []
    for g in heads:
        s = score_ref[g]
        top = jnp.maximum(top_ref[g], jnp.max(s, axis=0, keepdims=True))
        w = jnp.exp2(s - top)
        rescale = jnp.exp2(top_ref[g] - top)
        new_top_ref[g] = top
        new_total_ref[g] = rescale * total_ref[g] + jnp.sum(w, axis=0, keepdims=True)
        weight_ref[g] = w.astype(jnp.bfloat16)
        rescales.append(rescale)
    for g in heads:
        new_sum_ref[g] = rescales[g] * sum_ref[g] + weighted(kv_refs, g, weight_ref[g])


def far_kernel(scale, steps, q_ref, bias_ref, top_ref, total_ref, sum_ref, *refs):
    kv_refs = refs[: len(steps)]
    out_ref, score_ref, weight_ref, part_ref, held, sem = refs[len(steps) :]
    rows = q_ref.shape[0]
    bias = bias_of(bias_ref, steps, rows)
    width = QUERY_PER_KEY * HEAD_WIDTH
    heads = range(sum_ref.shape[0])
    for g in heads:
        score_ref[g] = scores_of(q_ref, kv_refs, g, bias, scale)
    rescales, inverses = [], []
    for g in heads:
        s = score_ref[g]
        top = jnp.maximum(top_ref[g], jnp.max(s, axis=0, keepdims=True))
        w = jnp.exp2(s - top)
        rescale = jnp.exp2(top_ref[g] - top)
        inverse = 1.0 / (rescale * total_ref[g] + jnp.sum(w, axis=0, keepdims=True))
        weight_ref[g] = w.astype(jnp.bfloat16)
        rescales.append(rescale * inverse)
        inverses.append(inverse)
    for g in heads:
        part_ref[g] = weighted(kv_refs, g, weight_ref[g]) * inverses[g]
    copies = []
    for g in heads:
        o = (rescales[g] * sum_ref[g] + part_ref[g]).T.astype(held.dtype)
        for j in range(QUERY_PER_KEY):
            held[g, :, j * HEAD_WIDTH : (j + 1) * HEAD_WIDTH] = o[j * rows : (j + 1) * rows]
        copy = pltpu.make_async_copy(held.at[g], out_ref.at[:, pl.ds(g * width, width)], sem.at[g])
        copy.start()
        copies.append(copy)
    for copy in copies:
        copy.wait()


def local(queries, keys, values, doc_lengths):
    rows, width = keys.shape
    key_heads = width // HEAD_WIDTH
    steps = MAXDOC // rows
    blocks = lax.axis_size("outer") * lax.axis_size("inner")
    count = 4 * blocks
    device_of = {chunk_of(d, blocks): d for d in range(count)}
    own = pl.pallas_call(
        join_kernel,
        out_shape=jax.ShapeDtypeStruct((2 * rows, width), keys.dtype),
        in_specs=[HBM, HBM],
        out_specs=ANY,
        scratch_shapes=[pltpu.SemaphoreType.DMA((2,))],
        compiler_params=PARAMS,
        name="join",
    )(in_hbm(keys), in_hbm(values))
    got = {0: own}
    for step in SENT:
        pairs = [(device_of[k], device_of[k + step]) for k in range(count - step)]
        got[step] = lax.ppermute(own, AXES, pairs)

    block = lax.axis_index("outer") * lax.axis_size("inner") + lax.axis_index("inner")
    part = lax.axis_index("head")
    chunk = jnp.where(part < 2, 2 * block + part, count - 4 - 2 * block + part)
    base = jnp.reshape(chunk * rows, (1,)).astype(jnp.int32)
    scale = math.log2(math.e) / math.sqrt(HEAD_WIDTH)
    heads_rows = QUERY_PER_KEY * rows
    row = jax.ShapeDtypeStruct((key_heads, 1, heads_rows), jnp.float32)
    sums = jax.ShapeDtypeStruct((key_heads, HEAD_WIDTH, heads_rows), jnp.float32)

    def cost(chunks):
        pairs = chunks * rows * heads_rows * key_heads
        return pl.CostEstimate(flops=4 * HEAD_WIDTH * pairs, bytes_accessed=1_000_000, transcendentals=pairs)

    def scratch(chunks):
        shape = (key_heads, chunks * rows, heads_rows)
        return [pltpu.VMEM(shape, jnp.float32), pltpu.VMEM(shape, jnp.bfloat16)]

    q, bias, *state = pl.pallas_call(
        functools.partial(near_kernel, scale, NEAR),
        out_shape=(
            jax.ShapeDtypeStruct(queries.shape, queries.dtype),
            jax.ShapeDtypeStruct(((steps + 1) * rows, LANES), jnp.float32),
            row,
            row,
            sums,
        ),
        in_specs=[SMEM, VMEM, HBM] + [VMEM] * len(NEAR),
        out_specs=(VMEM,) * 5,
        scratch_shapes=[pltpu.SemaphoreType.DMA],
        cost_estimate=cost(len(NEAR)),
        compiler_params=PARAMS,
        name="near",
    )(base, doc_lengths.reshape(-1, LANES), in_hbm(queries), *[got[n] for n in NEAR])
    for mid in MIDS:
        state = pl.pallas_call(
            functools.partial(mid_kernel, scale, mid),
            out_shape=(row, row, sums),
            in_specs=[VMEM] * (5 + len(mid)),
            out_specs=(VMEM,) * 3,
            scratch_shapes=scratch(len(mid)),
            cost_estimate=cost(len(mid)),
            compiler_params=PARAMS,
            name="mid",
        )(q, bias, *state, *[got[n] for n in mid])
    return pl.pallas_call(
        functools.partial(far_kernel, scale, FAR),
        out_shape=jax.ShapeDtypeStruct(queries.shape, queries.dtype),
        in_specs=[VMEM] * (5 + len(FAR)),
        out_specs=ANY,
        scratch_shapes=scratch(len(FAR))
        + [
            pltpu.VMEM((key_heads, HEAD_WIDTH, heads_rows), jnp.float32),
            pltpu.VMEM((key_heads, rows, QUERY_PER_KEY * HEAD_WIDTH), queries.dtype),
            pltpu.SemaphoreType.DMA((key_heads,)),
        ],
        cost_estimate=cost(len(FAR)),
        compiler_params=PARAMS,
        name="far",
    )(q, bias, *state, *[got[n] for n in FAR])


def solution(mesh):
    return jax.shard_map(
        local,
        mesh=mesh,
        in_specs=(P(AXES, None), P(AXES, None), P(AXES, None), P()),
        out_specs=P(AXES, None),
        check_vma=False,
    )
```

```python
import functools
import math

import jax
import jax.numpy as jnp
from jax import lax
from jax.experimental import pallas as pl
from jax.experimental.pallas import tpu as pltpu
from jax.sharding import PartitionSpec as P

HEAD_WIDTH = 128
QUERY_PER_KEY = 8
MAXDOC = 256
LANES = 128
NEG = -1e30
SENT = (3, 2, 1, 4)
NEAR = (3, 0)
MIDS = ((2,),)
FAR = (1, 4)
AXES = ("outer", "inner", "head")
VMEM = pl.BlockSpec(memory_space=pltpu.VMEM)
SMEM = pl.BlockSpec(memory_space=pltpu.SMEM)
ANY = pl.BlockSpec(memory_space=pl.ANY)
HBM = pl.BlockSpec(memory_space=pltpu.HBM)
PARAMS = pltpu.CompilerParams(vmem_limit_bytes=16 << 20)


def in_hbm(array):
    return pltpu.with_memory_space_constraint(array, pltpu.HBM)


def chunk_of(device, blocks):
    block, part = divmod(device, 4)
    return 2 * block + part if part < 2 else 4 * blocks - 4 - 2 * block + part


def join_kernel(k_ref, v_ref, out_ref, sem):
    rows = k_ref.shape[0]
    copies = [
        pltpu.make_async_copy(k_ref, out_ref.at[pl.ds(0, rows)], sem.at[0]),
        pltpu.make_async_copy(v_ref, out_ref.at[pl.ds(rows, rows)], sem.at[1]),
    ]
    for copy in copies:
        copy.start()
    for copy in copies:
        copy.wait()


def first_positions(base, lengths, rows):
    ends = lengths
    lane = lax.broadcasted_iota(jnp.int32, ends.shape, 1)
    shift = 1
    while shift < LANES:
        ends = ends + jnp.where(lane >= shift, pltpu.roll(ends, shift, 1), 0)
        shift *= 2
    totals = jnp.broadcast_to(ends[:, LANES - 1 :], ends.shape)
    row = lax.broadcasted_iota(jnp.int32, ends.shape, 0)
    above = jnp.where(row >= 1, pltpu.roll(totals, 1, 0), 0)
    shift = 1
    while shift < ends.shape[0]:
        above = above + jnp.where(row >= shift, pltpu.roll(above, shift, 0), 0)
        shift *= 2
    ends = ends + above
    own = base + lax.broadcasted_iota(jnp.int32, (rows, LANES), 0)
    first = jnp.zeros((rows, LANES), jnp.int32)
    for i in range(ends.shape[0]):
        end = jnp.broadcast_to(ends[i : i + 1, :], (rows, LANES))
        first = jnp.maximum(first, jnp.where(end <= own, end, 0))
    first = jnp.broadcast_to(jnp.max(first, axis=1, keepdims=True), (rows, LANES))
    return jnp.concatenate([first] * (LANES // rows), axis=0).T


def queries_of(q_ref, g):
    start = g * QUERY_PER_KEY * HEAD_WIDTH
    return jnp.concatenate(
        [q_ref[:, start + j * HEAD_WIDTH : start + (j + 1) * HEAD_WIDTH] for j in range(QUERY_PER_KEY)],
        axis=0,
    )


def part_of(refs, half, g):
    rows = refs[0].shape[0] // 2
    return jnp.concatenate(
        [r[half * rows : (half + 1) * rows, g * HEAD_WIDTH : (g + 1) * HEAD_WIDTH] for r in refs], axis=0
    )


def bias_of(bias_ref, steps, rows):
    count = bias_ref.shape[0]
    return jnp.concatenate([bias_ref[count - (n + 1) * rows : count - n * rows] for n in steps], axis=0)


def scores_of(q_ref, refs, g, bias, scale):
    q = q_ref[g]
    s = lax.dot_general(
        part_of(refs, 0, g), q, (((1,), (1,)), ((), ())), preferred_element_type=jnp.float32
    )
    return s * scale + jnp.concatenate([bias] * (q.shape[0] // LANES), axis=1)


def weighted(refs, g, w):
    return lax.dot_general(
        part_of(refs, 1, g),
        w,
        (((0,), (0,)), ((), ())),
        preferred_element_type=jnp.float32,
    )


def near_kernel(scale, near, base_ref, len_ref, q_hbm_ref, *refs):
    kv_refs = refs[: len(near)]
    q_ref, bias_ref, top_ref, total_ref, sum_ref, held, sem = refs[len(near) :]
    copy = pltpu.make_async_copy(q_hbm_ref, held, sem)
    copy.start()
    rows = held.shape[0]
    base = base_ref[0]
    first = first_positions(base, len_ref[...], rows)
    count = bias_ref.shape[0]
    first = jnp.broadcast_to(first[:1], (count, LANES))
    lane = lax.broadcasted_iota(jnp.int32, (count, LANES), 1)
    column = lax.broadcasted_iota(jnp.int32, (count, LANES), 0) + (base + rows - count)
    bias_ref[...] = jnp.where((column >= first) & (column <= base + lane % rows), 0.0, NEG)
    bias = bias_of(bias_ref, near, rows)
    copy.wait()
    for g in range(sum_ref.shape[0]):
        q_ref[g] = queries_of(held, g)
        s = scores_of(q_ref, kv_refs, g, bias, scale)
        top = jnp.max(s, axis=0, keepdims=True)
        w = jnp.exp2(s - top)
        top_ref[g] = top
        total_ref[g] = jnp.sum(w, axis=0, keepdims=True)
        sum_ref[g] = weighted(kv_refs, g, w.astype(jnp.bfloat16))


def mid_kernel(scale, steps, q_ref, bias_ref, top_ref, total_ref, sum_ref, *refs):
    kv_refs = refs[: len(steps)]
    new_top_ref, new_total_ref, new_sum_ref, score_ref, weight_ref = refs[len(steps) :]
    bias = bias_of(bias_ref, steps, q_ref.shape[1] // QUERY_PER_KEY)
    heads = range(sum_ref.shape[0])
    for g in heads:
        score_ref[g] = scores_of(q_ref, kv_refs, g, bias, scale)
    rescales = []
    for g in heads:
        s = score_ref[g]
        top = jnp.maximum(top_ref[g], jnp.max(s, axis=0, keepdims=True))
        w = jnp.exp2(s - top)
        rescale = jnp.exp2(top_ref[g] - top)
        new_top_ref[g] = top
        new_total_ref[g] = rescale * total_ref[g] + jnp.sum(w, axis=0, keepdims=True)
        weight_ref[g] = w.astype(jnp.bfloat16)
        rescales.append(rescale)
    for g in heads:
        new_sum_ref[g] = rescales[g] * sum_ref[g] + weighted(kv_refs, g, weight_ref[g])


def far_kernel(scale, steps, q_ref, bias_ref, top_ref, total_ref, sum_ref, *refs):
    kv_refs = refs[: len(steps)]
    out_ref, score_ref, weight_ref, part_ref, held, sem = refs[len(steps) :]
    rows = q_ref.shape[1] // QUERY_PER_KEY
    bias = bias_of(bias_ref, steps, rows)
    half = QUERY_PER_KEY // 2
    heads = range(sum_ref.shape[0])
    for g in heads:
        score_ref[g] = scores_of(q_ref, kv_refs, g, bias, scale)
    rescales, inverses = [], []
    for g in heads:
        s = score_ref[g]
        top = jnp.maximum(top_ref[g], jnp.max(s, axis=0, keepdims=True))
        w = jnp.exp2(s - top)
        rescale = jnp.exp2(top_ref[g] - top)
        inverse = 1.0 / (rescale * total_ref[g] + jnp.sum(w, axis=0, keepdims=True))
        weight_ref[g] = w.astype(jnp.bfloat16)
        rescales.append(rescale * inverse)
        inverses.append(inverse)
    for g in heads:
        part_ref[g] = weighted(kv_refs, g, weight_ref[g]) * inverses[g]
    copies = []
    for g in heads:
        for n in range(2):
            lanes = slice(n * half * rows, (n + 1) * half * rows)
            o = (rescales[g][:, lanes] * sum_ref[g, :, lanes] + part_ref[g, :, lanes]).T
            o = jnp.concatenate([o[j * rows : (j + 1) * rows] for j in range(half)], axis=1)
            held[2 * g + n] = o.astype(held.dtype)
            at = pl.ds((2 * g + n) * half * HEAD_WIDTH, half * HEAD_WIDTH)
            copy = pltpu.make_async_copy(held.at[2 * g + n], out_ref.at[:, at], sem.at[2 * g + n])
            copy.start()
            copies.append(copy)
    for copy in copies:
        copy.wait()


def local(queries, keys, values, doc_lengths):
    rows, width = keys.shape
    key_heads = width // HEAD_WIDTH
    steps = MAXDOC // rows
    blocks = lax.axis_size("outer") * lax.axis_size("inner")
    count = 4 * blocks
    device_of = {chunk_of(d, blocks): d for d in range(count)}
    own = pl.pallas_call(
        join_kernel,
        out_shape=jax.ShapeDtypeStruct((2 * rows, width), keys.dtype),
        in_specs=[HBM, HBM],
        out_specs=ANY,
        scratch_shapes=[pltpu.SemaphoreType.DMA((2,))],
        compiler_params=PARAMS,
        name="join",
    )(in_hbm(keys), in_hbm(values))
    got = {0: own}
    for step in SENT:
        pairs = [(device_of[k], device_of[k + step]) for k in range(count - step)]
        got[step] = lax.ppermute(own, AXES, pairs)

    block = lax.axis_index("outer") * lax.axis_size("inner") + lax.axis_index("inner")
    part = lax.axis_index("head")
    chunk = jnp.where(part < 2, 2 * block + part, count - 4 - 2 * block + part)
    base = jnp.reshape(chunk * rows, (1,)).astype(jnp.int32)
    scale = math.log2(math.e) / math.sqrt(HEAD_WIDTH)
    heads_rows = QUERY_PER_KEY * rows
    row = jax.ShapeDtypeStruct((key_heads, 1, heads_rows), jnp.float32)
    sums = jax.ShapeDtypeStruct((key_heads, HEAD_WIDTH, heads_rows), jnp.float32)

    def cost(chunks):
        pairs = chunks * rows * heads_rows * key_heads
        return pl.CostEstimate(flops=4 * HEAD_WIDTH * pairs, bytes_accessed=1_000_000, transcendentals=pairs)

    def scratch(chunks):
        shape = (key_heads, chunks * rows, heads_rows)
        return [pltpu.VMEM(shape, jnp.float32), pltpu.VMEM(shape, jnp.bfloat16)]

    q, bias, *state = pl.pallas_call(
        functools.partial(near_kernel, scale, NEAR),
        out_shape=(
            jax.ShapeDtypeStruct((key_heads, heads_rows, HEAD_WIDTH), queries.dtype),
            jax.ShapeDtypeStruct(((steps + 1) * rows, LANES), jnp.float32),
            row,
            row,
            sums,
        ),
        in_specs=[SMEM, VMEM, HBM] + [VMEM] * len(NEAR),
        out_specs=(VMEM,) * 5,
        scratch_shapes=[pltpu.VMEM(queries.shape, queries.dtype), pltpu.SemaphoreType.DMA],
        cost_estimate=cost(len(NEAR)),
        compiler_params=PARAMS,
        name="near",
    )(base, doc_lengths.reshape(-1, LANES), in_hbm(queries), *[got[n] for n in NEAR])
    for mid in MIDS:
        state = pl.pallas_call(
            functools.partial(mid_kernel, scale, mid),
            out_shape=(row, row, sums),
            in_specs=[VMEM] * (5 + len(mid)),
            out_specs=(VMEM,) * 3,
            scratch_shapes=scratch(len(mid)),
            cost_estimate=cost(len(mid)),
            compiler_params=PARAMS,
            name="mid",
        )(q, bias, *state, *[got[n] for n in mid])
    return pl.pallas_call(
        functools.partial(far_kernel, scale, FAR),
        out_shape=jax.ShapeDtypeStruct(queries.shape, queries.dtype),
        in_specs=[VMEM] * (5 + len(FAR)),
        out_specs=ANY,
        scratch_shapes=scratch(len(FAR))
        + [
            pltpu.VMEM((key_heads, HEAD_WIDTH, heads_rows), jnp.float32),
            pltpu.VMEM((2 * key_heads, rows, QUERY_PER_KEY // 2 * HEAD_WIDTH), queries.dtype),
            pltpu.SemaphoreType.DMA((2 * key_heads,)),
        ],
        cost_estimate=cost(len(FAR)),
        compiler_params=PARAMS,
        name="far",
    )(q, bias, *state, *[got[n] for n in FAR])


def solution(mesh):
    return jax.shard_map(
        local,
        mesh=mesh,
        in_specs=(P(AXES, None), P(AXES, None), P(AXES, None), P()),
        out_specs=P(AXES, None),
        check_vma=False,
    )
```
